256 devices in a mesh: chaos: 64 (over z, y, core), mesh: 4 (over x).
Axes of the slice: x: 4, y: 4, z: 8, core: 2. Of those that a mesh axis runs over, the one named last changes fastest.
Arguments:
- coefficients: bfloat16 [128, 96, 320], P('mesh', None, 'chaos'), may hold values from -6 to 6
- stiffness: bfloat16 [11, 12288, 6, 96], P(None, ('mesh', 'chaos')), may hold values from -0.25 to 0.25
- columns: int32 [128, 6], P('mesh'), may hold values from 0 to 127
- pair_rows: int32 [11, 1280], replicated, may hold values from 0 to 319
- pair_cols: int32 [11, 1280], replicated, may hold values from 0 to 319
- pair_vals: float32 [11, 1280], replicated, may hold values from -2 to 2
Outputs:
- applied: bfloat16 [128, 96, 320], P('mesh', None, 'chaos')
The draws below stay inside these ranges and needn't reach their ends.
All inputs are finite; a program needn't handle non-finite values.
Results may differ from the reference program's by a relative error of at most 0.001.
Values may be sent and summed in bfloat16 or wider, within the bound.
No kernel may reach another device: no remote copies, remote signals or barrier semaphores. Data moves between devices by JAX's collectives and lax.ppermute only.
A program may use at most 128 MiB of HBM per device.

```python
import jax
import jax.numpy as jnp
from jax import lax

BLOCK = 96
MODES = 11
P_SIZE = 320
NNZ = 6
NODES = 128
PAIRS = 1280


def place_ends(entries, stream_key, least, largest):
    extent = entries.shape
    index_at = [jax.random.randint(jax.random.fold_in(stream_key, axis), (), 0, extent[axis]) for axis in range(len(extent))]
    entries = entries.at[tuple(index_at)].set(least)
    longest = extent.index(max(extent))
    index_at[longest] = (index_at[longest] + 1) % extent[longest]
    return entries.at[tuple(index_at)].set(largest)


def block_scale(stream_key, extent, pieces, low, top_value):
    level, own = 1.0, jax.random.fold_in(stream_key, 6)
    for axis_at, blocks in pieces:
        heights = jnp.exp(jax.random.uniform(jax.random.fold_in(own, axis_at), (blocks,), jnp.float32, low / len(pieces), top_value / len(pieces)))
        level = level * jnp.repeat(heights, extent[axis_at] // blocks).reshape([-1 if axis == axis_at else 1 for axis in range(len(extent))])
    return level


def normal_values(stream_key, shape, spread, bound, shards=(), kind=jnp.bfloat16):
    factor_of = block_scale(stream_key, shape, shards, -0.22, 0.18) if shards else 1.0
    array = jax.random.normal(stream_key, shape, jnp.float32) * spread * factor_of
    return jnp.minimum(jnp.maximum(array, -bound), bound).astype(kind)


def setup_inputs(seed: int = 0) -> dict:
    key_of = jax.random.split(jax.random.key(seed), 7)
    return {
        "coefficients": normal_values(key_of[0], (NODES, BLOCK, P_SIZE), 1.0, 6.0, ((0, 4), (2, 64))),
        "stiffness": normal_values(key_of[1], (MODES, NODES * BLOCK, NNZ, BLOCK), (NNZ * BLOCK) ** -0.5, 0.25, ((1, 256),)),
        "columns": place_ends(jax.random.randint(key_of[2], (NODES, NNZ), 0, NODES), jax.random.fold_in(key_of[2], 1), 0, NODES - 1).astype(jnp.int32),
        "pair_rows": place_ends(jax.random.randint(key_of[3], (MODES, PAIRS), 0, P_SIZE), jax.random.fold_in(key_of[3], 1), 0, P_SIZE - 1).astype(jnp.int32),
        "pair_cols": place_ends(jax.random.randint(key_of[4], (MODES, PAIRS), 0, P_SIZE), jax.random.fold_in(key_of[4], 1), 0, P_SIZE - 1).astype(jnp.int32),
        "pair_vals": normal_values(key_of[5], (MODES, PAIRS), 0.15, 2.0, (), jnp.float32),
    }


def reference(coefficients, stiffness, columns, pair_rows, pair_cols, pair_vals):
    mode_index = jnp.broadcast_to(jnp.arange(MODES, dtype=jnp.int32)[:, None], pair_rows.shape)
    coupling = jnp.zeros((MODES, P_SIZE, P_SIZE), jnp.float32).at[mode_index, pair_cols, pair_rows].add(pair_vals.astype(jnp.float32))
    picked = coefficients[columns].astype(jnp.float32)
    blocks = stiffness.reshape(MODES, NODES, BLOCK, NNZ, BLOCK)
    applied = jnp.zeros((NODES, BLOCK, P_SIZE), jnp.float32)
    for mode in range(MODES):
        products = jnp.einsum('rasb,rsbj->raj', blocks[mode].astype(jnp.float32), picked)
        applied = applied + jnp.einsum('raj,ji->rai', products, coupling[mode], precision=lax.Precision.HIGHEST)
    return applied.astype(jnp.bfloat16)
```

```python
import jax
import jax.numpy as jnp
from jax import lax
from jax.experimental import pallas as pl
from jax.experimental.pallas import tpu as pltpu
from jax.sharding import Mesh, PartitionSpec as P

LANES = 128
BF16 = jnp.bfloat16
F32 = jnp.float32


def split_two(value):
    high = value.astype(BF16)
    return high, (value - high.astype(F32)).astype(BF16)


def call(body, name, outs, scratch=(), **specs):
    return pl.pallas_call(
        body,
        out_shape=outs,
        scratch_shapes=scratch,
        compiler_params=pltpu.CompilerParams(vmem_limit_bytes=40 << 20),
        name=name,
        **specs,
    )


def coupling_kernel(own, parts, rows_ref, cols_ref, vals_ref, high_ref, low_ref, total_ref):
    modes, pairs = rows_ref.shape
    half = own * parts
    total_ref[...] = jnp.zeros_like(total_ref)
    out_iota = lax.broadcasted_iota(jnp.int32, (2 * half, pairs), 0)
    in_iota = lax.broadcasted_iota(jnp.int32, (2 * LANES, pairs), 0)
    for mode in range(modes):
        first = mode * half
        base = first // LANES * LANES
        rows = rows_ref[mode : mode + 1, :]
        cols = cols_ref[mode : mode + 1, :] + (first - base)
        vals = vals_ref[mode : mode + 1, :]
        high, low = split_two(vals)
        every_row = jnp.where(out_iota == rows, 1.0, 0.0).astype(BF16)
        hit = in_iota == cols
        w_high = jnp.where(hit, high.astype(F32), 0.0).astype(BF16)
        w_low = jnp.where(hit, low.astype(F32), 0.0).astype(BF16)
        dims = (((1,), (1,)), ((), ()))
        got = lax.dot_general(every_row, w_high, dims, preferred_element_type=F32)
        got += lax.dot_general(every_row, w_low, dims, preferred_element_type=F32)
        total_ref[:, base : base + 2 * LANES] += got
    high_ref[...], low_ref[...] = split_two(total_ref[...])


def rows_kernel(core_ref, mine_ref, theirs_ref, out_ref):
    modes, slots, rows, block = mine_ref.shape
    core = core_ref[0]
    out_ref[...] = jnp.zeros_like(out_ref)
    for ref, at in ((mine_ref, core), (theirs_ref, 1 - core)):
        for mode in range(modes):
            for slot in range(slots):
                start = pl.multiple_of(at * rows, 16)
                out_ref[mode, pl.ds(start, rows), slot * LANES : slot * LANES + block] = ref[mode, slot]


def select_kernel(target_ref, out_ref):
    count, width = out_ref.shape
    lanes = lax.broadcasted_iota(jnp.int32, (count, width), 1)
    out_ref[...] = jnp.where(lanes == target_ref[...], 1.0, 0.0).astype(BF16)


def send_kernel(select_ref, a_ref, b_ref, c_ref, d_ref, out_ref):
    own, nodes, block = a_ref.shape
    held = jnp.concatenate(
        [ref[...].reshape(own * nodes, block) for ref in (a_ref, b_ref, c_ref, d_ref)], axis=0
    )
    got = jnp.dot(select_ref[...], held, preferred_element_type=F32).astype(BF16)
    out_ref[...] = jnp.zeros_like(out_ref)
    out_ref[:, :block] = got


def apply_kernel(own, slots, got_ref, rows_ref, high_ref, low_ref, mine_ref, theirs_ref, wide, slotted, stacked):
    parts, unit, _ = got_ref.shape
    modes = rows_ref.shape[0]
    half = own * parts
    wide[: parts * unit, :] = got_ref[...].reshape(parts * unit, LANES).astype(F32)
    wide[parts * unit :, :] = jnp.zeros((8, LANES), F32)
    for slot in range(slots):
        for part in range(parts):
            slotted[slot, pl.ds(own * part, 8), :] = wide[pl.ds(unit * part + own * slot, 8), :]
    held = jnp.concatenate([slotted[slot, :half, :].astype(BF16) for slot in range(slots)], axis=1)
    products = lax.dot_general(
        held, rows_ref[...].reshape(modes * LANES, slots * LANES), (((1,), (1,)), ((), ())), preferred_element_type=F32
    )
    stacked[:, modes * half :, :] = jnp.zeros_like(stacked[:, modes * half :, :])
    for mode in range(modes):
        high, low = split_two(products[:, mode * LANES : (mode + 1) * LANES])
        stacked[0, mode * half : (mode + 1) * half, :] = high
        stacked[1, mode * half : (mode + 1) * half, :] = low
    high = stacked[0]
    total = jnp.dot(high_ref[...], high, preferred_element_type=F32)
    total += jnp.dot(high_ref[...], stacked[1], preferred_element_type=F32)
    total += jnp.dot(low_ref[...], high, preferred_element_type=F32)
    mine_ref[...] = total[:half]
    theirs_ref[...] = total[half:]


def finish_kernel(own, mine_ref, other_ref, out_ref, total):
    parts = out_ref.shape[0]
    half = own * parts
    total[:half, :] = mine_ref[...] + other_ref[...]
    total[half:, :] = jnp.zeros((8, LANES), F32)
    for part in range(parts):
        out_ref[part] = total[pl.ds(own * part, 8), :].astype(BF16)


def deliver_kernel(got_ref, out_ref, wide):
    own, nodes, block = out_ref.shape
    wide[...] = got_ref[...].reshape(nodes * 8, LANES).astype(F32)
    for i in range(own):
        out_ref[i] = wide[pl.ds(i, nodes, stride=8), :][:, :block].astype(BF16)


def local(coefficients, stiffness, columns, pair_rows, pair_cols, pair_vals):
    nodes, block, own = coefficients.shape
    modes, rows, slots, _ = stiffness.shape
    pairs = pair_rows.shape[1]
    parts = lax.axis_size("chip")
    meshes = lax.axis_size("mesh")
    half = own * parts
    unit = 32
    core = lax.axis_index("core")
    me = lax.axis_index("mesh")

    swap = [(0, 1), (1, 0)]
    mine = jnp.transpose(stiffness, (0, 2, 1, 3))
    theirs = lax.ppermute(mine, "core", swap)

    held = jnp.transpose(coefficients, (2, 0, 1))
    around = [held] + [
        lax.ppermute(held, "mesh", [(i, (i + d) % meshes) for i in range(meshes)]) for d in range(1, meshes)
    ]

    place = lax.rem(me - columns // nodes + meshes, meshes) * (own * nodes) + columns % nodes
    place = place[:, :, None] + (nodes * lax.iota(jnp.int32, own))[None, None, :]
    place = jnp.pad(place.reshape(parts, slots * own), ((0, 0), (0, unit - slots * own)), constant_values=-1)
    select = call(select_kernel, "select", jax.ShapeDtypeStruct((parts * unit, meshes * own * nodes), BF16))(
        place.reshape(parts * unit, 1)
    )
    outgoing = call(send_kernel, "send", jax.ShapeDtypeStruct((parts * unit, LANES), BF16))(select, *around)
    got = lax.all_to_all(outgoing.reshape(parts, unit, LANES), "chip", 0, 0, tiled=True)

    def share(index):
        part = index // (2 * own)
        rest = index - part * (2 * own)
        other = jnp.where(rest >= own, 1, 0)
        return part * own + rest - other * own, other

    row_at, row_core = share(pair_rows)
    col_at, col_core = share(pair_cols)
    row_at = row_at + jnp.where(row_core == core, 0, half)
    col_at = jnp.where(col_core == core, col_at, 4 * LANES)
    width = (modes * half + LANES - 1) // LANES * LANES
    high, low = call(
        lambda *refs: coupling_kernel(own, parts, *refs),
        "coupling",
        [jax.ShapeDtypeStruct((2 * half, width), BF16)] * 2,
        [pltpu.VMEM((2 * half, width), F32)],
    )(row_at, col_at, pair_vals)

    all_rows = call(
        rows_kernel,
        "rows",
        jax.ShapeDtypeStruct((modes, LANES, slots * LANES), BF16),
        in_specs=[pl.BlockSpec(memory_space=pltpu.SMEM)] + [pl.BlockSpec(memory_space=pltpu.VMEM)] * 2,
    )(core.reshape(1).astype(jnp.int32), mine, theirs)

    partial, other = call(
        lambda *refs: apply_kernel(own, slots, *refs),
        "apply",
        [jax.ShapeDtypeStruct((half, LANES), F32)] * 2,
        [
            pltpu.VMEM((parts * unit + 8, LANES), F32),
            pltpu.VMEM((slots, half + 8, LANES), F32),
            pltpu.VMEM((2, width, LANES), BF16),
        ],
    )(got, all_rows, high, low)
    other = lax.ppermute(other, "core", swap)
    finished = call(
        lambda *refs: finish_kernel(own, *refs),
        "finish",
        jax.ShapeDtypeStruct((parts, 8, LANES), BF16),
        [pltpu.VMEM((half + 8, LANES), F32)],
    )(partial, other)
    returned = lax.all_to_all(finished, "chip", 0, 0, tiled=True)
    out = call(
        deliver_kernel,
        "deliver",
        jax.ShapeDtypeStruct((own, nodes, block), BF16),
        [pltpu.VMEM((nodes * 8, LANES), F32)],
    )(returned)
    return jnp.transpose(out, (1, 2, 0))


def solution(mesh):
    chaos, meshes = mesh.devices.shape
    chips = Mesh(mesh.devices.reshape(chaos // 2, 2, meshes), ("chip", "core", "mesh"))
    spread = ("chip", "core")
    return jax.shard_map(
        local,
        mesh=chips,
        in_specs=(
            P("mesh", None, spread),
            P(None, ("mesh", *spread), None, None),
            P("mesh", None),
            P(),
            P(),
            P(),
        ),
        out_specs=P("mesh", None, spread),
        check_vma=False,
    )
```

```python
import math

import jax
import jax.numpy as jnp
from jax import lax
from jax.experimental import pallas as pl
from jax.experimental.pallas import tpu as pltpu
from jax.sharding import Mesh, PartitionSpec as P


LANES = 128
BF16 = jnp.bfloat16
F32 = jnp.float32


def split_two(value):
    high = value.astype(BF16)
    return high, (value - high.astype(F32)).astype(BF16)


def call(body, outs, scratch=(), vmem=12, **specs):
    return pl.pallas_call(
        body,
        out_shape=outs,
        scratch_shapes=scratch,
        compiler_params=pltpu.CompilerParams(vmem_limit_bytes=vmem << 20),
        **specs,
    )


def in_hbm(array):
    return pltpu.with_memory_space_constraint(array, pltpu.HBM)


NT = (((1,), (1,)), ((), ()))


def sublane_iota(count, width):
    return lax.broadcasted_iota(jnp.int32, (count, width), 0).astype(F32).astype(BF16)


def spans(modes, half):
    step = LANES // math.gcd(LANES, half)
    starts = range(0, modes, step)
    return [(k, min(k + step, modes), -(-(min(k + step, modes) - k) * half // LANES) * LANES) for k in starts]


def prepare_kernel(half, groups, where_ref, near_ref, far_ref, cols_ref, high_ref, low_ref, mine_hbm, theirs, *refs):
    count = len(groups)
    couplings, rows_out = refs[:count], refs[count]
    totals, splits = refs[count + 1 : 2 * count + 1], refs[2 * count + 1 : 3 * count + 1]
    every_row, weights, mine, in_sem, out_sem = refs[3 * count + 1 :]
    modes, slots, rows, block = mine.shape
    pairs = cols_ref.shape[1]
    load = pltpu.make_async_copy(mine_hbm, mine, in_sem)
    load.start()
    one, zero = jnp.ones((), BF16), jnp.zeros((), BF16)
    iota = sublane_iota(half, pairs)
    stores = []
    for group, (first, last, _) in enumerate(groups):
        total = totals[group]
        if last == modes:
            total[...] = jnp.zeros_like(total)
        for mode in range(first, last):
            at, slot = slice(mode, mode + 1), mode % 2
            hit = iota == cols_ref[at, :]
            weights[slot, :half, :] = jnp.where(hit, high_ref[at, :], zero)
            weights[slot, half:, :] = jnp.where(hit, low_ref[at, :], zero)
            for side, ref in enumerate((near_ref, far_ref)):
                every_row[slot, side * half : (side + 1) * half, :] = jnp.where(iota == ref[at, :], one, zero)
            got = lax.dot_general(every_row[slot], weights[slot, :half], NT, preferred_element_type=F32)
            got += lax.dot_general(every_row[slot], weights[slot, half:], NT, preferred_element_type=F32)
            total[:, (mode - first) * half : (mode - first + 1) * half] = got
        splits[group][0], splits[group][1] = split_two(total[...])
        store = pltpu.make_async_copy(splits[group], couplings[group], out_sem.at[group])
        store.start()
        stores.append(store)
        if group == 0:
            core = where_ref[1]
            rows_out[...] = jnp.zeros_like(rows_out)
            load.wait()
            for ref, part in ((mine, core), (theirs, 1 - core)):
                start = pl.multiple_of(part * rows, 16)
                for mode in range(modes):
                    for slot in range(slots):
                        lanes = slice(slot * LANES, slot * LANES + block)
                        rows_out[mode, pl.ds(start, rows), lanes] = ref[mode, slot]
    for store in stores:
        store.wait()


def tables_kernel(own, where_ref, *refs):
    (held_hbm, *tables_hbm), (held_ref, out_ref, near_ref, far_ref, at_ref, high_ref, low_ref) = refs[:5], refs[5:12]
    columns_ref, rows_ref, cols_ref, vals_ref, table, sem = refs[12:]
    targets = (columns_ref, rows_ref, cols_ref, vals_ref, held_ref)
    loads = [
        pltpu.make_async_copy(hbm, target, sem.at[at])
        for at, (hbm, target) in enumerate(zip((*tables_hbm, held_hbm), targets))
    ]
    for load in loads:
        load.start()
    for load in loads:
        load.wait()
    me, core = where_ref[0], where_ref[1]
    slots, nodes = columns_ref.shape
    columns = columns_ref[...]
    bits = nodes.bit_length() - 1
    away = jnp.bitwise_and(me - jnp.right_shift(columns, bits), LANES // nodes - 1)
    place = away * nodes + jnp.bitwise_and(columns, nodes - 1)
    table[...] = jnp.zeros_like(table)
    table[:slots, :nodes] = place.astype(F32)
    upright = table[...].T
    lanes = lax.broadcasted_iota(jnp.int32, (nodes, LANES), 1).astype(F32)
    for slot in range(slots):
        hit = upright[:nodes, slot : slot + 1] == lanes
        out_ref[slot * nodes : (slot + 1) * nodes, :] = jnp.where(hit, 1.0, 0.0).astype(BF16)

    def share(index):
        part = jnp.right_shift(index * (65536 // (2 * own) + 1), 16)
        rest = index - part * (2 * own)
        other = jnp.where(rest >= own, 1, 0)
        return (part * own + rest - other * own).astype(F32), other == core

    row_at, row_mine = share(rows_ref[...])
    col_at, col_mine = share(cols_ref[...])
    near_ref[...] = jnp.where(row_mine, row_at, -1.0).astype(BF16)
    far_ref[...] = jnp.where(row_mine, -1.0, row_at).astype(BF16)
    at_ref[...] = jnp.where(col_mine, col_at, -1.0).astype(BF16)
    high_ref[...], low_ref[...] = split_two(vals_ref[...])


def send_kernel(unit, select_ref, a_ref, b_ref, c_ref, d_ref, out_ref, held, wide):
    own, nodes, block = a_ref.shape
    slots = select_ref.shape[0] // nodes
    held[...] = jnp.zeros_like(held)
    for ref_at, ref in enumerate((a_ref, b_ref, c_ref, d_ref)):
        for i in range(own):
            held[i, ref_at * nodes : (ref_at + 1) * nodes, :block] = ref[i]
    select = select_ref[...]
    for i in range(own):
        got = jnp.dot(select, held[i], preferred_element_type=F32)
        for slot in range(slots):
            wide[pl.ds(own * slot + i, nodes, stride=unit), :] = got[slot * nodes : (slot + 1) * nodes]
    for line in range(own * slots, unit):
        wide[pl.ds(line, nodes, stride=unit), :] = jnp.zeros((nodes, LANES), F32)
    out_ref[...] = wide[...].astype(BF16)


def apply_kernel(own, slots, groups, got_ref, rows_ref, *refs):
    count = len(groups)
    couplings, (mine_ref, theirs_ref, wide, slotted), refs = refs[:count], refs[count : count + 4], refs[count + 4 :]
    splits, stacks, sem = refs[:count], refs[count : 2 * count], refs[2 * count]
    loads = [pltpu.make_async_copy(couplings[at], splits[at], sem.at[at]) for at in range(count)]
    for load in loads:
        load.start()
    parts, unit, _ = got_ref.shape
    half = own * parts
    wide[: parts * unit, :] = got_ref[...].reshape(parts * unit, LANES).astype(F32)
    wide[parts * unit :, :] = jnp.zeros((8, LANES), F32)
    for slot in range(slots):
        for part in range(parts):
            slotted[slot, pl.ds(own * part, 8), :] = wide[pl.ds(unit * part + own * slot, 8), :]
    held = jnp.concatenate([slotted[slot, :half, :].astype(BF16) for slot in range(slots)], axis=1)
    total = jnp.zeros((2 * half, LANES), F32)
    for at, (first, last, width) in enumerate(groups):
        lines = (last - first) * LANES
        some_rows = rows_ref[first:last].reshape(lines, slots * LANES)
        products = lax.dot_general(held, some_rows, NT, preferred_element_type=F32)
        stack = stacks[at]
        if (last - first) * half < width:
            stack[(last - first) * half :, :] = jnp.zeros_like(stack[(last - first) * half :, :])
        for mode in range(last - first):
            high, low = split_two(products[:, mode * LANES : (mode + 1) * LANES])
            stack[mode * half : (mode + 1) * half, :LANES] = high
            stack[mode * half : (mode + 1) * half, LANES:] = low
    for at in range(count):
        loads[at].wait()
        both = jnp.dot(splits[at][0], stacks[at][...], preferred_element_type=F32)
        total += both[:, :LANES] + both[:, LANES:]
        total += jnp.dot(splits[at][1], stacks[at][:, :LANES], preferred_element_type=F32)
    mine_ref[...] = total[:half]
    theirs_ref[...] = total[half:]


def finish_kernel(own, mine_ref, other_ref, out_ref, total):
    parts = out_ref.shape[0]
    half = own * parts
    total[:half, :] = mine_ref[...] + other_ref[...]
    total[half:, :] = jnp.zeros((8, LANES), F32)
    for part in range(parts):
        out_ref[part] = total[pl.ds(own * part, 8), :].astype(BF16)


def deliver_kernel(got_ref, out_ref, wide):
    own, nodes, block = out_ref.shape
    wide[...] = got_ref[...].reshape(nodes * 8, LANES).astype(F32)
    for i in range(own):
        out_ref[i] = wide[pl.ds(i, nodes, stride=8), :][:, :block].astype(BF16)


def compute(coefficients, stiffness, columns, pair_rows, pair_cols, pair_vals):
    nodes, block, own = coefficients.shape
    modes, _, slots, _ = stiffness.shape
    pairs = pair_rows.shape[1]
    parts = lax.axis_size("chip")
    meshes = lax.axis_size("mesh")
    half = own * parts
    unit = 32
    where = jnp.stack([lax.axis_index("mesh"), lax.axis_index("core")]).astype(jnp.int32)

    swap = [(0, 1), (1, 0)]
    held = jnp.transpose(coefficients, (2, 0, 1))
    around = {}
    for d in (2, 1, 3):
        around[d] = lax.ppermute(held, "mesh", [(i, (i + d) % meshes) for i in range(meshes)])
    smem = pl.BlockSpec(memory_space=pltpu.SMEM)
    vmem = pl.BlockSpec(memory_space=pltpu.VMEM)
    hbm = pl.BlockSpec(memory_space=pltpu.HBM)
    entries = jax.ShapeDtypeStruct((modes, pairs), BF16)
    held, select, *tables = call(
        lambda *refs: tables_kernel(own, *refs),
        [jax.ShapeDtypeStruct(held.shape, BF16), jax.ShapeDtypeStruct((slots * nodes, LANES), BF16)] + [entries] * 5,
        [pltpu.VMEM((slots, nodes), jnp.int32)]
        + [pltpu.VMEM((modes, pairs), x.dtype) for x in (pair_rows, pair_cols, pair_vals)]
        + [pltpu.VMEM((8, LANES), F32), pltpu.SemaphoreType.DMA((5,))],
        in_specs=[smem] + [hbm] * 5,
    )(where, *map(in_hbm, (held, columns.T, pair_rows, pair_cols, pair_vals)))
    mine = jnp.transpose(stiffness, (0, 2, 1, 3))
    mine, select = lax.optimization_barrier((mine, select))
    theirs = lax.ppermute(mine, "core", swap)
    outgoing = call(
        lambda *refs: send_kernel(unit, *refs),
        jax.ShapeDtypeStruct((parts * unit, LANES), BF16),
        [pltpu.VMEM((own, LANES, LANES), BF16), pltpu.VMEM((parts * unit, LANES), F32)],
    )(select, held, *(around[d] for d in (1, 2, 3)))
    got = lax.all_to_all(outgoing.reshape(parts, unit, LANES), "chip", 0, 0, tiled=True)

    groups = spans(modes, half)
    pieces = [(2, 2 * half, width) for _, _, width in groups]
    *couplings, all_rows = call(
        lambda *refs: prepare_kernel(half, groups, *refs),
        [pltpu.HBM(piece, BF16) for piece in pieces]
        + [jax.ShapeDtypeStruct((modes, LANES, slots * LANES), BF16)],
        [pltpu.VMEM(piece[1:], F32) for piece in pieces]
        + [pltpu.VMEM(piece, BF16) for piece in pieces]
        + [pltpu.VMEM((2, 2 * half, pairs), BF16)] * 2
        + [pltpu.VMEM(mine.shape, BF16)]
        + [pltpu.SemaphoreType.DMA, pltpu.SemaphoreType.DMA((len(groups),))],
        in_specs=[smem] + [vmem] * 5 + [hbm, vmem],
        out_specs=[hbm] * len(groups) + [vmem],
        vmem=32,
    )(where, *tables, in_hbm(mine), theirs)

    partial, other = call(
        lambda *refs: apply_kernel(own, slots, groups, *refs),
        [jax.ShapeDtypeStruct((half, LANES), F32)] * 2,
        [pltpu.VMEM((parts * unit + 8, LANES), F32), pltpu.VMEM((slots, half + 8, LANES), F32)]
        + [pltpu.VMEM(piece, BF16) for piece in pieces]
        + [pltpu.VMEM((piece[2], 2 * LANES), BF16) for piece in pieces]
        + [pltpu.SemaphoreType.DMA((len(groups),))],
        in_specs=[vmem] * 2 + [hbm] * len(groups),
        out_specs=[vmem] * 2,
        vmem=32,
    )(got, all_rows, *map(in_hbm, couplings))
    other = lax.ppermute(other, "core", swap)
    finished = call(
        lambda *refs: finish_kernel(own, *refs),
        jax.ShapeDtypeStruct((parts, 8, LANES), BF16),
        [pltpu.VMEM((half + 8, LANES), F32)],
    )(partial, other)
    returned = lax.all_to_all(finished, "chip", 0, 0, tiled=True)
    out = call(
        deliver_kernel, jax.ShapeDtypeStruct((own, nodes, block), BF16), [pltpu.VMEM((nodes * 8, LANES), F32)]
    )(returned)
    return jnp.transpose(out, (1, 2, 0))


def solution(mesh):
    chaos, meshes = mesh.devices.shape
    chips = Mesh(mesh.devices.reshape(chaos // 2, 2, meshes), ("chip", "core", "mesh"))
    spread = ("chip", "core")
    return jax.shard_map(
        compute,
        mesh=chips,
        in_specs=(
            P("mesh", None, spread),
            P(None, ("mesh", *spread), None, None),
            P("mesh", None),
            P(),
            P(),
            P(),
        ),
        out_specs=P("mesh", None, spread),
        check_vma=False,
    )
```

```python
import jax
import jax.numpy as jnp
from jax import lax
from jax.experimental import pallas as pl
from jax.experimental.pallas import tpu as pltpu
from jax.sharding import Mesh, PartitionSpec as P


LANES = 128
BF16 = jnp.bfloat16
F32 = jnp.float32


def split_two(value):
    high = value.astype(BF16)
    return high, (value - high.astype(F32)).astype(BF16)


def call(body, outs, scratch=(), vmem=12, **specs):
    return pl.pallas_call(
        body,
        out_shape=outs,
        scratch_shapes=scratch,
        compiler_params=pltpu.CompilerParams(vmem_limit_bytes=vmem << 20),
        **specs,
    )


def in_hbm(array):
    return pltpu.with_memory_space_constraint(array, pltpu.HBM)


TAIL = 3 * LANES
NT = (((1,), (1,)), ((), ()))


def sublane_iota(count, width):
    return lax.broadcasted_iota(jnp.int32, (count, width), 0).astype(F32).astype(BF16)


def prepare_kernel(half, near_ref, far_ref, cols_ref, high_ref, low_ref, out_ref, every_row, weights):
    modes, pairs = cols_ref.shape
    one, zero = jnp.ones((), BF16), jnp.zeros((), BF16)
    iota = sublane_iota(half, pairs)
    for mode in range(modes):
        at, slot = slice(mode, mode + 1), mode % 2
        hit = iota == cols_ref[at, :]
        weights[slot, :half, :] = jnp.where(hit, high_ref[at, :], zero)
        weights[slot, half:, :] = jnp.where(hit, low_ref[at, :], zero)
        for side, ref in enumerate((near_ref, far_ref)):
            every_row[slot, side * half : (side + 1) * half, :] = jnp.where(iota == ref[at, :], one, zero)
        got = lax.dot_general(weights[slot], every_row[slot], NT, preferred_element_type=F32)
        high, low = split_two(got[:half] + got[half:])
        lines = slice(mode * half, (mode + 1) * half)
        out_ref[lines, : 2 * half] = high
        out_ref[lines, 2 * half : TAIL] = low[:, 2 * LANES :]
        out_ref[lines, TAIL:] = low[:, : 2 * LANES]


def tables_kernel(own, where_ref, *refs):
    (held_hbm, *tables_hbm), (held_ref, out_ref, near_ref, far_ref, at_ref, high_ref, low_ref) = refs[:5], refs[5:12]
    columns_ref, rows_ref, cols_ref, vals_ref, table, sem = refs[12:]
    targets = (columns_ref, rows_ref, cols_ref, vals_ref, held_ref)
    loads = [
        pltpu.make_async_copy(hbm, target, sem.at[at])
        for at, (hbm, target) in enumerate(zip((*tables_hbm, held_hbm), targets))
    ]
    for load in loads:
        load.start()
    for load in loads:
        load.wait()
    me, core = where_ref[0], where_ref[1]
    slots, nodes = columns_ref.shape
    columns = columns_ref[...]
    bits = nodes.bit_length() - 1
    away = jnp.bitwise_and(me - jnp.right_shift(columns, bits), LANES // nodes - 1)
    place = away * nodes + jnp.bitwise_and(columns, nodes - 1)
    table[...] = jnp.zeros_like(table)
    table[:slots, :nodes] = place.astype(F32)
    upright = table[...].T
    lanes = lax.broadcasted_iota(jnp.int32, (nodes, LANES), 1).astype(F32)
    for slot in range(slots):
        hit = upright[:nodes, slot : slot + 1] == lanes
        out_ref[slot * nodes : (slot + 1) * nodes, :] = jnp.where(hit, 1.0, 0.0).astype(BF16)

    def share(index):
        part = jnp.right_shift(index * (65536 // (2 * own) + 1), 16)
        rest = index - part * (2 * own)
        other = jnp.where(rest >= own, 1, 0)
        return (part * own + rest - other * own).astype(F32), other == core

    row_at, row_mine = share(rows_ref[...])
    col_at, col_mine = share(cols_ref[...])
    near_ref[...] = jnp.where(row_mine, row_at, -1.0).astype(BF16)
    far_ref[...] = jnp.where(row_mine, -1.0, row_at).astype(BF16)
    at_ref[...] = jnp.where(col_mine, col_at, -1.0).astype(BF16)
    high_ref[...], low_ref[...] = split_two(vals_ref[...])


def send_kernel(unit, select_ref, a_ref, b_ref, c_ref, d_ref, out_ref, held, wide):
    own, nodes, block = a_ref.shape
    slots = select_ref.shape[0] // nodes
    held[...] = jnp.zeros_like(held)
    for ref_at, ref in enumerate((a_ref, b_ref, c_ref, d_ref)):
        for i in range(own):
            held[i, ref_at * nodes : (ref_at + 1) * nodes, :block] = ref[i]
    select = select_ref[...]
    for i in range(own):
        got = jnp.dot(select, held[i], preferred_element_type=F32)
        for slot in range(slots):
            wide[pl.ds(own * slot + i, nodes, stride=unit), :] = got[slot * nodes : (slot + 1) * nodes]
    for line in range(own * slots, unit):
        wide[pl.ds(line, nodes, stride=unit), :] = jnp.zeros((nodes, LANES), F32)
    out_ref[...] = wide[...].astype(BF16)


def apply_kernel(own, where_ref, got_ref, theirs_ref, coupling_ref, mine_hbm, near_ref, far_ref, mine, wide, slotted, stack, sem):
    load = pltpu.make_async_copy(mine_hbm, mine, sem)
    load.start()
    core = where_ref[1]
    parts, unit, _ = got_ref.shape
    modes, slots, rows, block = mine.shape
    half = own * parts
    wide[: parts * unit, :] = got_ref[...].reshape(parts * unit, LANES).astype(F32)
    wide[parts * unit :, :] = jnp.zeros((8, LANES), F32)
    for slot in range(slots):
        for part in range(parts):
            slotted[slot, pl.ds(own * part, 8), :] = wide[pl.ds(unit * part + own * slot, 8), :]
    held = [slotted[slot, :half, :block].astype(BF16) for slot in range(slots)]
    for ref, part in ((theirs_ref, 1 - core), (mine, core)):
        if ref is mine:
            load.wait()
        products = jnp.zeros((modes * rows, half), F32)
        for slot in range(slots):
            lines = ref[:, slot].reshape(modes * rows, block)
            products += lax.dot_general(lines, held[slot], NT, preferred_element_type=F32)
        start = pl.multiple_of(part * rows, 16)
        for mode in range(modes):
            high, low = split_two(products[mode * rows : (mode + 1) * rows])
            stack[mode, pl.ds(start, rows), :] = high
            stack[mode, pl.ds(2 * rows + start, rows), :] = low
    first = jnp.zeros((4 * rows, TAIL), F32)
    second = jnp.zeros((2 * rows, 2 * LANES), F32)
    for mode in range(modes):
        lines = slice(mode * half, (mode + 1) * half)
        first += jnp.dot(stack[mode], coupling_ref[lines, :TAIL], preferred_element_type=F32)
        second += jnp.dot(stack[mode, : 2 * rows], coupling_ref[lines, TAIL:], preferred_element_type=F32)
    both = first[: 2 * rows] + first[2 * rows :]
    tail = first[: 2 * rows, 2 * half :]
    total = jnp.concatenate([both[:, : 2 * LANES] + second, both[:, 2 * LANES : 2 * half] + tail], axis=1)
    edge = jnp.zeros((2 * rows, TAIL - 2 * half), F32)
    upright = jnp.concatenate([total, edge], axis=1).T
    near_ref[:, : 2 * rows] = upright[:half]
    far_ref[:, : 2 * rows] = upright[half : 2 * half]
    near_ref[:, 2 * rows :] = jnp.zeros((half, LANES - 2 * rows), F32)
    far_ref[:, 2 * rows :] = jnp.zeros((half, LANES - 2 * rows), F32)


def finish_kernel(own, mine_ref, other_ref, out_ref, total):
    parts = out_ref.shape[0]
    half = own * parts
    total[:half, :] = mine_ref[...] + other_ref[...]
    total[half:, :] = jnp.zeros((8, LANES), F32)
    for part in range(parts):
        out_ref[part] = total[pl.ds(own * part, 8), :].astype(BF16)


def deliver_kernel(got_ref, out_ref, wide):
    own, nodes, block = out_ref.shape
    wide[...] = got_ref[...].reshape(nodes * 8, LANES).astype(F32)
    for i in range(own):
        out_ref[i] = wide[pl.ds(i, nodes, stride=8), :][:, :block].astype(BF16)


def compute(coefficients, stiffness, columns, pair_rows, pair_cols, pair_vals):
    nodes, block, own = coefficients.shape
    modes, rows, slots, _ = stiffness.shape
    pairs = pair_rows.shape[1]
    parts = lax.axis_size("chip")
    meshes = lax.axis_size("mesh")
    half = own * parts
    unit = 32
    where = jnp.stack([lax.axis_index("mesh"), lax.axis_index("core")]).astype(jnp.int32)

    swap = [(0, 1), (1, 0)]
    held = jnp.transpose(coefficients, (2, 0, 1))
    around = {}
    for d in (2, 1, 3):
        around[d] = lax.ppermute(held, "mesh", [(i, (i + d) % meshes) for i in range(meshes)])
    smem = pl.BlockSpec(memory_space=pltpu.SMEM)
    vmem = pl.BlockSpec(memory_space=pltpu.VMEM)
    hbm = pl.BlockSpec(memory_space=pltpu.HBM)
    entries = jax.ShapeDtypeStruct((modes, pairs), BF16)
    held, select, *tables = call(
        lambda *refs: tables_kernel(own, *refs),
        [jax.ShapeDtypeStruct(held.shape, BF16), jax.ShapeDtypeStruct((slots * nodes, LANES), BF16)] + [entries] * 5,
        [pltpu.VMEM((slots, nodes), jnp.int32)]
        + [pltpu.VMEM((modes, pairs), x.dtype) for x in (pair_rows, pair_cols, pair_vals)]
        + [pltpu.VMEM((8, LANES), F32), pltpu.SemaphoreType.DMA((5,))],
        in_specs=[smem] + [hbm] * 5,
    )(where, *map(in_hbm, (held, columns.T, pair_rows, pair_cols, pair_vals)))
    outgoing = call(
        lambda *refs: send_kernel(unit, *refs),
        jax.ShapeDtypeStruct((parts * unit, LANES), BF16),
        [pltpu.VMEM((own, LANES, LANES), BF16), pltpu.VMEM((parts * unit, LANES), F32)],
    )(select, held, *(around[d] for d in (1, 2, 3)))
    got = lax.all_to_all(outgoing.reshape(parts, unit, LANES), "chip", 0, 0, tiled=True)

    mine = jnp.transpose(stiffness, (0, 2, 1, 3))
    theirs = lax.ppermute(mine, "core", swap)
    coupling = call(
        lambda *refs: prepare_kernel(half, *refs),
        jax.ShapeDtypeStruct((modes * half, TAIL + 2 * LANES), BF16),
        [pltpu.VMEM((2, 2 * half, pairs), BF16)] * 2,
    )(*tables)
    partial, other = call(
        lambda *refs: apply_kernel(own, *refs),
        [jax.ShapeDtypeStruct((half, LANES), F32)] * 2,
        [
            pltpu.VMEM(mine.shape, BF16),
            pltpu.VMEM((parts * unit + 8, LANES), F32),
            pltpu.VMEM((slots, half + 8, LANES), F32),
            pltpu.VMEM((modes, 4 * rows, half), BF16),
            pltpu.SemaphoreType.DMA,
        ],
        in_specs=[smem] + [vmem] * 3 + [hbm],
    )(where, got, theirs, coupling, in_hbm(mine))
    other = lax.ppermute(other, "core", swap)
    finished = call(
        lambda *refs: finish_kernel(own, *refs),
        jax.ShapeDtypeStruct((parts, 8, LANES), BF16),
        [pltpu.VMEM((half + 8, LANES), F32)],
    )(partial, other)
    returned = lax.all_to_all(finished, "chip", 0, 0, tiled=True)
    out = call(
        deliver_kernel, jax.ShapeDtypeStruct((own, nodes, block), BF16), [pltpu.VMEM((nodes * 8, LANES), F32)]
    )(returned)
    return jnp.transpose(out, (1, 2, 0))


def solution(mesh):
    chaos, meshes = mesh.devices.shape
    chips = Mesh(mesh.devices.reshape(chaos // 2, 2, meshes), ("chip", "core", "mesh"))
    spread = ("chip", "core")
    return jax.shard_map(
        compute,
        mesh=chips,
        in_specs=(
            P("mesh", None, spread),
            P(None, ("mesh", *spread), None, None),
            P("mesh", None),
            P(),
            P(),
            P(),
        ),
        out_specs=P("mesh", None, spread),
        check_vma=False,
    )
```

```python
import jax
import jax.numpy as jnp
from jax import lax
from jax.experimental import pallas as pl
from jax.experimental.pallas import tpu as pltpu
from jax.sharding import Mesh, PartitionSpec as P


LANES = 128
BF16 = jnp.bfloat16
F32 = jnp.float32


def split_two(value):
    high = value.astype(BF16)
    return high, (value - high.astype(F32)).astype(BF16)


def call(body, outs, scratch=(), vmem=12, **specs):
    return pl.pallas_call(
        body,
        out_shape=outs,
        scratch_shapes=scratch,
        compiler_params=pltpu.CompilerParams(vmem_limit_bytes=vmem << 20),
        **specs,
    )


def in_hbm(array):
    return pltpu.with_memory_space_constraint(array, pltpu.HBM)


TAIL = 3 * LANES
NT = (((1,), (1,)), ((), ()))


def sublane_iota(count, width):
    return lax.broadcasted_iota(jnp.int32, (count, width), 0).astype(F32).astype(BF16)


def prepare_kernel(half, near_ref, far_ref, cols_ref, high_ref, low_ref, out_ref, rest_hbm, every_row, weights, rest, sem):
    modes, pairs = cols_ref.shape
    one, zero = jnp.ones((), BF16), jnp.zeros((), BF16)
    iota = sublane_iota(half, pairs)
    stores = []
    for mode in range(modes):
        at, slot = slice(mode, mode + 1), mode % 2
        hit = iota == cols_ref[at, :]
        weights[slot, :half, :] = jnp.where(hit, high_ref[at, :], zero)
        weights[slot, half:, :] = jnp.where(hit, low_ref[at, :], zero)
        for side, ref in enumerate((near_ref, far_ref)):
            every_row[slot, side * half : (side + 1) * half, :] = jnp.where(iota == ref[at, :], one, zero)
        got = lax.dot_general(weights[slot], every_row[slot], NT, preferred_element_type=F32)
        high, low = split_two(got[:half] + got[half:])
        lines = slice(mode * half, (mode + 1) * half)
        out_ref[lines, : 2 * half] = high
        out_ref[lines, 2 * half :] = low[:, 2 * LANES :]
        rest[lines, :] = low[:, : 2 * LANES]
        store = pltpu.make_async_copy(rest.at[lines], rest_hbm.at[lines], sem.at[mode])
        store.start()
        stores.append(store)
    for store in stores:
        store.wait()


def tables_kernel(own, where_ref, *refs):
    (held_hbm, *tables_hbm), (held_ref, out_ref, near_ref, far_ref, at_ref, high_ref, low_ref) = refs[:5], refs[5:12]
    columns_ref, rows_ref, cols_ref, vals_ref, table, sem = refs[12:]
    targets = (columns_ref, rows_ref, cols_ref, vals_ref, held_ref)
    loads = [
        pltpu.make_async_copy(hbm, target, sem.at[at])
        for at, (hbm, target) in enumerate(zip((*tables_hbm, held_hbm), targets))
    ]
    for load in loads:
        load.start()
    for load in loads:
        load.wait()
    me, core = where_ref[0], where_ref[1]
    slots, nodes = columns_ref.shape
    columns = columns_ref[...]
    bits = nodes.bit_length() - 1
    away = jnp.bitwise_and((me - jnp.right_shift(columns, bits)) * (1 - 2 * core), LANES // nodes - 1)
    place = away * nodes + jnp.bitwise_and(columns, nodes - 1)
    table[...] = jnp.zeros_like(table)
    table[:slots, :nodes] = place.astype(F32)
    upright = table[...].T
    lanes = lax.broadcasted_iota(jnp.int32, (nodes, LANES), 1).astype(F32)
    for slot in range(slots):
        hit = upright[:nodes, slot : slot + 1] == lanes
        out_ref[slot * nodes : (slot + 1) * nodes, :] = jnp.where(hit, 1.0, 0.0).astype(BF16)

    def share(index):
        part = jnp.right_shift(index * (65536 // (2 * own) + 1), 16)
        rest = index - part * (2 * own)
        other = jnp.where(rest >= own, 1, 0)
        return (part * own + rest - other * own).astype(F32), other == core

    row_at, row_mine = share(rows_ref[...])
    col_at, col_mine = share(cols_ref[...])
    near_ref[...] = jnp.where(row_mine, row_at, -1.0).astype(BF16)
    far_ref[...] = jnp.where(row_mine, -1.0, row_at).astype(BF16)
    at_ref[...] = jnp.where(col_mine, col_at, -1.0).astype(BF16)
    high_ref[...], low_ref[...] = split_two(vals_ref[...])


def send_kernel(unit, select_ref, a_ref, b_ref, c_ref, d_ref, out_ref, held, wide):
    own, nodes, block = a_ref.shape
    slots = select_ref.shape[0] // nodes
    held[...] = jnp.zeros_like(held)
    for ref_at, ref in enumerate((a_ref, b_ref, c_ref, d_ref)):
        for i in range(own):
            held[i, ref_at * nodes : (ref_at + 1) * nodes, :block] = ref[i]
    select = select_ref[...]
    for i in range(own):
        got = jnp.dot(select, held[i], preferred_element_type=F32)
        for slot in range(slots):
            wide[pl.ds(own * slot + i, nodes, stride=unit), :] = got[slot * nodes : (slot + 1) * nodes]
    for line in range(own * slots, unit):
        wide[pl.ds(line, nodes, stride=unit), :] = jnp.zeros((nodes, LANES), F32)
    out_ref[...] = wide[...].astype(BF16)


def apply_kernel(own, where_ref, got_ref, theirs_ref, mine_ref, coupling_ref, rest_hbm, near_ref, far_ref, rest, wide, slotted, stack, sem):
    load = pltpu.make_async_copy(rest_hbm, rest, sem)
    load.start()
    core = where_ref[1]
    parts, unit, _ = got_ref.shape
    modes, slots, rows, block = mine_ref.shape
    half = own * parts
    wide[: parts * unit, :] = got_ref[...].reshape(parts * unit, LANES).astype(F32)
    wide[parts * unit :, :] = jnp.zeros((8, LANES), F32)
    for slot in range(slots):
        for part in range(parts):
            slotted[slot, pl.ds(own * part, 8), :] = wide[pl.ds(unit * part + own * slot, 8), :]
    held = [slotted[slot, :half, :block].astype(BF16) for slot in range(slots)]
    for ref, part in ((theirs_ref, 1 - core), (mine_ref, core)):
        products = jnp.zeros((modes * rows, half), F32)
        for slot in range(slots):
            lines = ref[:, slot].reshape(modes * rows, block)
            products += lax.dot_general(lines, held[slot], NT, preferred_element_type=F32)
        start = pl.multiple_of(part * rows, 16)
        for mode in range(modes):
            high, low = split_two(products[mode * rows : (mode + 1) * rows])
            stack[mode, pl.ds(start, rows), :] = high
            stack[mode, pl.ds(2 * rows + start, rows), :] = low
    first = jnp.zeros((4 * rows, TAIL), F32)
    second = jnp.zeros((2 * rows, 2 * LANES), F32)
    for mode in range(modes):
        lines = slice(mode * half, (mode + 1) * half)
        first += jnp.dot(stack[mode], coupling_ref[lines, :], preferred_element_type=F32)
    load.wait()
    for mode in range(modes):
        lines = slice(mode * half, (mode + 1) * half)
        second += jnp.dot(stack[mode, : 2 * rows], rest[lines, :], preferred_element_type=F32)
    both = first[: 2 * rows] + first[2 * rows :]
    tail = first[: 2 * rows, 2 * half :]
    total = jnp.concatenate([both[:, : 2 * LANES] + second, both[:, 2 * LANES : 2 * half] + tail], axis=1)
    edge = jnp.zeros((2 * rows, TAIL - 2 * half), F32)
    upright = jnp.concatenate([total, edge], axis=1).T
    near_ref[:, : 2 * rows] = upright[:half]
    far_ref[:, : 2 * rows] = upright[half : 2 * half]
    near_ref[:, 2 * rows :] = jnp.zeros((half, LANES - 2 * rows), F32)
    far_ref[:, 2 * rows :] = jnp.zeros((half, LANES - 2 * rows), F32)


def finish_kernel(own, mine_ref, other_ref, out_ref, total):
    parts = out_ref.shape[0]
    half = own * parts
    total[:half, :] = mine_ref[...] + other_ref[...]
    total[half:, :] = jnp.zeros((8, LANES), F32)
    for part in range(parts):
        out_ref[part] = total[pl.ds(own * part, 8), :].astype(BF16)


def deliver_kernel(got_ref, out_ref, wide):
    own, nodes, block = out_ref.shape
    wide[...] = got_ref[...].reshape(nodes * 8, LANES).astype(F32)
    for i in range(own):
        out_ref[i] = wide[pl.ds(i, nodes, stride=8), :][:, :block].astype(BF16)


def compute(coefficients, stiffness, columns, pair_rows, pair_cols, pair_vals):
    nodes, block, own = coefficients.shape
    modes, rows, slots, _ = stiffness.shape
    pairs = pair_rows.shape[1]
    parts = lax.axis_size("chip")
    meshes = lax.axis_size("mesh")
    half = own * parts
    unit = 32
    where = jnp.stack([lax.axis_index("mesh"), lax.axis_index("core")]).astype(jnp.int32)

    swap = [(0, 1), (1, 0)]
    held = jnp.transpose(coefficients, (2, 0, 1))

    def turn(block, way):
        ways = [(c * meshes + m, c * meshes + (m + (way if c == 0 else -way)) % meshes) for c in range(2) for m in range(meshes)]
        return lax.ppermute(block, ("core", "mesh"), ways)

    behind = turn(held, 1)
    ahead = turn(held, -1)
    across = turn(behind, 1)
    smem = pl.BlockSpec(memory_space=pltpu.SMEM)
    vmem = pl.BlockSpec(memory_space=pltpu.VMEM)
    hbm = pl.BlockSpec(memory_space=pltpu.HBM)
    entries = jax.ShapeDtypeStruct((modes, pairs), BF16)
    held, select, *tables = call(
        lambda *refs: tables_kernel(own, *refs),
        [jax.ShapeDtypeStruct(held.shape, BF16), jax.ShapeDtypeStruct((slots * nodes, LANES), BF16)] + [entries] * 5,
        [pltpu.VMEM((slots, nodes), jnp.int32)]
        + [pltpu.VMEM((modes, pairs), x.dtype) for x in (pair_rows, pair_cols, pair_vals)]
        + [pltpu.VMEM((8, LANES), F32), pltpu.SemaphoreType.DMA((5,))],
        in_specs=[smem] + [hbm] * 5,
    )(where, *map(in_hbm, (held, columns.T, pair_rows, pair_cols, pair_vals)))
    outgoing = call(
        lambda *refs: send_kernel(unit, *refs),
        jax.ShapeDtypeStruct((parts * unit, LANES), BF16),
        [pltpu.VMEM((own, LANES, LANES), BF16), pltpu.VMEM((parts * unit, LANES), F32)],
    )(select, held, behind, across, ahead)
    got = lax.all_to_all(outgoing.reshape(parts, unit, LANES), "chip", 0, 0, tiled=True)

    mine = jnp.transpose(stiffness, (0, 2, 1, 3))
    theirs = lax.ppermute(mine, "core", swap)
    coupling, rest = call(
        lambda *refs: prepare_kernel(half, *refs),
        [jax.ShapeDtypeStruct((modes * half, TAIL), BF16), pltpu.HBM((modes * half, 2 * LANES), BF16)],
        [
            *[pltpu.VMEM((2, 2 * half, pairs), BF16)] * 2,
            pltpu.VMEM((modes * half, 2 * LANES), BF16),
            pltpu.SemaphoreType.DMA((modes,)),
        ],
        out_specs=[vmem, hbm],
    )(*tables)
    partial, other = call(
        lambda *refs: apply_kernel(own, *refs),
        [jax.ShapeDtypeStruct((half, LANES), F32)] * 2,
        [
            pltpu.VMEM((modes * half, 2 * LANES), BF16),
            pltpu.VMEM((parts * unit + 8, LANES), F32),
            pltpu.VMEM((slots, half + 8, LANES), F32),
            pltpu.VMEM((modes, 4 * rows, half), BF16),
            pltpu.SemaphoreType.DMA,
        ],
        in_specs=[smem] + [vmem] * 4 + [hbm],
    )(where, got, theirs, mine, coupling, in_hbm(rest))
    other = lax.ppermute(other, "core", swap)
    finished = call(
        lambda *refs: finish_kernel(own, *refs),
        jax.ShapeDtypeStruct((parts, 8, LANES), BF16),
        [pltpu.VMEM((half + 8, LANES), F32)],
    )(partial, other)
    returned = lax.all_to_all(finished, "chip", 0, 0, tiled=True)
    out = call(
        deliver_kernel, jax.ShapeDtypeStruct((own, nodes, block), BF16), [pltpu.VMEM((nodes * 8, LANES), F32)]
    )(returned)
    return jnp.transpose(out, (1, 2, 0))


def solution(mesh):
    chaos, meshes = mesh.devices.shape
    chips = Mesh(mesh.devices.reshape(chaos // 2, 2, meshes), ("chip", "core", "mesh"))
    spread = ("chip", "core")
    return jax.shard_map(
        compute,
        mesh=chips,
        in_specs=(
            P("mesh", None, spread),
            P(None, ("mesh", *spread), None, None),
            P("mesh", None),
            P(),
            P(),
            P(),
        ),
        out_specs=P("mesh", None, spread),
        check_vma=False,
    )
```

```python
import jax
import jax.numpy as jnp
from jax import lax
from jax.experimental import pallas as pl
from jax.experimental.pallas import tpu as pltpu
from jax.sharding import Mesh, PartitionSpec as P


LANES = 128
BF16 = jnp.bfloat16
F32 = jnp.float32


def split_two(value):
    high = value.astype(BF16)
    return high, (value - high.astype(F32)).astype(BF16)


def call(body, outs, scratch=(), vmem=12, **specs):
    return pl.pallas_call(
        body,
        out_shape=outs,
        scratch_shapes=scratch,
        compiler_params=pltpu.CompilerParams(vmem_limit_bytes=vmem << 20),
        **specs,
    )


def in_hbm(array):
    return pltpu.with_memory_space_constraint(array, pltpu.HBM)


TAIL = 3 * LANES
PIECES = 5
KEPT = 1
NT = (((1,), (1,)), ((), ()))


def sublane_iota(count, width):
    return lax.broadcasted_iota(jnp.int32, (count, width), 0).astype(F32).astype(BF16)


def prepare_kernel(half, near_ref, far_ref, cols_ref, high_ref, low_ref, out_ref, rest_hbm, kept_ref, every_row, weights, rest, sem):
    modes, pairs = cols_ref.shape
    one, zero = jnp.ones((), BF16), jnp.zeros((), BF16)
    iota = sublane_iota(half, pairs)
    stores = []
    for mode in range(modes):
        at, slot = slice(mode, mode + 1), mode % 2
        hit = iota == cols_ref[at, :]
        weights[slot, :half, :] = jnp.where(hit, high_ref[at, :], zero)
        weights[slot, half:, :] = jnp.where(hit, low_ref[at, :], zero)
        for side, ref in enumerate((near_ref, far_ref)):
            every_row[slot, side * half : (side + 1) * half, :] = jnp.where(iota == ref[at, :], one, zero)
        got = lax.dot_general(weights[slot], every_row[slot], NT, preferred_element_type=F32)
        high, low = split_two(got[:half] + got[half:])
        lines = slice(mode * half, (mode + 1) * half)
        out_ref[lines, : 2 * half] = high
        out_ref[lines, 2 * half :] = low[:, 2 * LANES :]
        if mode >= modes - KEPT:
            kept = mode - modes + KEPT
            kept_ref[kept * half : (kept + 1) * half, :] = low[:, : 2 * LANES]
            continue
        rest[lines, :] = low[:, : 2 * LANES]
        store = pltpu.make_async_copy(rest.at[lines], rest_hbm.at[lines], sem.at[mode])
        store.start()
        stores.append(store)
    for store in stores:
        store.wait()


def tables_kernel(own, where_ref, *refs):
    (held_hbm, *tables_hbm), (held_ref, out_ref, near_ref, far_ref, at_ref, high_ref, low_ref) = refs[:5], refs[5:12]
    columns_ref, rows_ref, cols_ref, vals_ref, table, sem = refs[12:]
    targets = (columns_ref, rows_ref, cols_ref, vals_ref, held_ref)
    loads = [
        pltpu.make_async_copy(hbm, target, sem.at[at])
        for at, (hbm, target) in enumerate(zip((*tables_hbm, held_hbm), targets))
    ]
    for load in loads:
        load.start()
    for load in loads:
        load.wait()
    me, core = where_ref[0], where_ref[1]
    slots, nodes = columns_ref.shape
    columns = columns_ref[...]
    bits = nodes.bit_length() - 1
    away = jnp.bitwise_and(me - jnp.right_shift(columns, bits), LANES // nodes - 1)
    place = away * nodes + jnp.bitwise_and(columns, nodes - 1)
    table[...] = jnp.zeros_like(table)
    table[:slots, :nodes] = place.astype(F32)
    upright = table[...].T
    lanes = lax.broadcasted_iota(jnp.int32, (nodes, LANES), 1).astype(F32)
    for slot in range(slots):
        hit = upright[:nodes, slot : slot + 1] == lanes
        out_ref[slot * nodes : (slot + 1) * nodes, :] = jnp.where(hit, 1.0, 0.0).astype(BF16)

    def share(index):
        part = jnp.right_shift(index * (65536 // (2 * own) + 1), 16)
        rest = index - part * (2 * own)
        other = jnp.where(rest >= own, 1, 0)
        return (part * own + rest - other * own).astype(F32), other == core

    row_at, row_mine = share(rows_ref[...])
    col_at, col_mine = share(cols_ref[...])
    near_ref[...] = jnp.where(row_mine, row_at, -1.0).astype(BF16)
    far_ref[...] = jnp.where(row_mine, -1.0, row_at).astype(BF16)
    at_ref[...] = jnp.where(col_mine, col_at, -1.0).astype(BF16)
    high_ref[...], low_ref[...] = split_two(vals_ref[...])


def send_kernel(unit, select_ref, a_ref, b_ref, c_ref, d_ref, out_ref, held, wide):
    own, nodes, block = a_ref.shape
    slots = select_ref.shape[0] // nodes
    held[...] = jnp.zeros_like(held)
    for ref_at, ref in enumerate((a_ref, b_ref, c_ref, d_ref)):
        for i in range(own):
            held[i, ref_at * nodes : (ref_at + 1) * nodes, :block] = ref[i]
    select = select_ref[...]
    for i in range(own):
        got = jnp.dot(select, held[i], preferred_element_type=F32)
        for slot in range(slots):
            wide[pl.ds(own * slot + i, nodes, stride=unit), :] = got[slot * nodes : (slot + 1) * nodes]
    for line in range(own * slots, unit):
        wide[pl.ds(line, nodes, stride=unit), :] = jnp.zeros((nodes, LANES), F32)
    out_ref[...] = wide[...].astype(BF16)


def apply_kernel(own, where_ref, got_ref, theirs_ref, mine_ref, coupling_ref, kept_ref, rest_hbm, near_ref, far_ref, rest, wide, slotted, stack, sem):
    pieces = sem.shape[0]
    length = rest.shape[0] // pieces

    def load(piece):
        at = pl.ds(pl.multiple_of(piece * length, 16), length)
        return pltpu.make_async_copy(rest_hbm.at[at], rest.at[at], sem.at[piece])

    @pl.loop(0, pieces)
    def _(piece):
        load(piece).start()

    core = where_ref[1]
    parts, unit, _ = got_ref.shape
    modes, slots, rows, block = mine_ref.shape
    half = own * parts
    wide[: parts * unit, :] = got_ref[...].reshape(parts * unit, LANES).astype(F32)
    wide[parts * unit :, :] = jnp.zeros((8, LANES), F32)
    for slot in range(slots):
        for part in range(parts):
            slotted[slot, pl.ds(own * part, 8), :] = wide[pl.ds(unit * part + own * slot, 8), :]
    held = [slotted[slot, :half, :block].astype(BF16) for slot in range(slots)]
    for ref, part in ((theirs_ref, 1 - core), (mine_ref, core)):
        products = jnp.zeros((modes * rows, half), F32)
        for slot in range(slots):
            lines = ref[:, slot].reshape(modes * rows, block)
            products += lax.dot_general(lines, held[slot], NT, preferred_element_type=F32)
        start = pl.multiple_of(part * rows, 16)
        for mode in range(modes):
            high, low = split_two(products[mode * rows : (mode + 1) * rows])
            stack[mode, pl.ds(start, rows), :] = high
            stack[mode, pl.ds(2 * rows + start, rows), :] = low
    first = jnp.zeros((4 * rows, TAIL), F32)
    second = jnp.zeros((2 * rows, 2 * LANES), F32)
    for mode in range(modes):
        lines = slice(mode * half, (mode + 1) * half)
        first += jnp.dot(stack[mode], coupling_ref[lines, :], preferred_element_type=F32)
    for kept in range(KEPT):
        low = kept_ref[kept * half : (kept + 1) * half, :]
        second += jnp.dot(stack[modes - KEPT + kept, : 2 * rows], low, preferred_element_type=F32)
    for piece in range(pieces):
        load(piece).wait()
    for mode in range(modes - KEPT):
        low = rest[mode * half : (mode + 1) * half, :]
        second += jnp.dot(stack[mode, : 2 * rows], low, preferred_element_type=F32)
    both = first[: 2 * rows] + first[2 * rows :]
    tail = first[: 2 * rows, 2 * half :]
    total = jnp.concatenate([both[:, : 2 * LANES] + second, both[:, 2 * LANES : 2 * half] + tail], axis=1)
    edge = jnp.zeros((2 * rows, TAIL - 2 * half), F32)
    upright = jnp.concatenate([total, edge], axis=1).T
    near_ref[:, : 2 * rows] = upright[:half]
    far_ref[:, : 2 * rows] = upright[half : 2 * half]
    near_ref[:, 2 * rows :] = jnp.zeros((half, LANES - 2 * rows), F32)
    far_ref[:, 2 * rows :] = jnp.zeros((half, LANES - 2 * rows), F32)


def finish_kernel(own, mine_ref, other_ref, out_ref, total):
    parts = out_ref.shape[0]
    half = own * parts
    total[:half, :] = mine_ref[...] + other_ref[...]
    total[half:, :] = jnp.zeros((8, LANES), F32)
    for part in range(parts):
        out_ref[part] = total[pl.ds(own * part, 8), :].astype(BF16)


def deliver_kernel(got_ref, out_ref, wide):
    own, nodes, block = out_ref.shape
    wide[...] = got_ref[...].reshape(nodes * 8, LANES).astype(F32)
    for i in range(own):
        out_ref[i] = wide[pl.ds(i, nodes, stride=8), :][:, :block].astype(BF16)


def compute(coefficients, stiffness, columns, pair_rows, pair_cols, pair_vals):
    nodes, block, own = coefficients.shape
    modes, rows, slots, _ = stiffness.shape
    pairs = pair_rows.shape[1]
    parts = lax.axis_size("chip")
    meshes = lax.axis_size("mesh")
    half = own * parts
    unit = 32
    where = jnp.stack([lax.axis_index("mesh"), lax.axis_index("core")]).astype(jnp.int32)

    swap = [(0, 1), (1, 0)]
    held = jnp.transpose(coefficients, (2, 0, 1))
    around = {}
    for d in (2, 1, 3):
        around[d] = lax.ppermute(held, "mesh", [(i, (i + d) % meshes) for i in range(meshes)])
    smem = pl.BlockSpec(memory_space=pltpu.SMEM)
    vmem = pl.BlockSpec(memory_space=pltpu.VMEM)
    hbm = pl.BlockSpec(memory_space=pltpu.HBM)
    entries = jax.ShapeDtypeStruct((modes, pairs), BF16)
    held, select, *tables = call(
        lambda *refs: tables_kernel(own, *refs),
        [jax.ShapeDtypeStruct(held.shape, BF16), jax.ShapeDtypeStruct((slots * nodes, LANES), BF16)] + [entries] * 5,
        [pltpu.VMEM((slots, nodes), jnp.int32)]
        + [pltpu.VMEM((modes, pairs), x.dtype) for x in (pair_rows, pair_cols, pair_vals)]
        + [pltpu.VMEM((8, LANES), F32), pltpu.SemaphoreType.DMA((5,))],
        in_specs=[smem] + [hbm] * 5,
    )(where, *map(in_hbm, (held, columns.T, pair_rows, pair_cols, pair_vals)))
    outgoing = call(
        lambda *refs: send_kernel(unit, *refs),
        jax.ShapeDtypeStruct((parts * unit, LANES), BF16),
        [pltpu.VMEM((own, LANES, LANES), BF16), pltpu.VMEM((parts * unit, LANES), F32)],
    )(select, held, *(around[d] for d in (1, 2, 3)))
    got = lax.all_to_all(outgoing.reshape(parts, unit, LANES), "chip", 0, 0, tiled=True)

    mine = jnp.transpose(stiffness, (0, 2, 1, 3))
    theirs = lax.ppermute(mine, "core", swap)
    coupling, rest, kept = call(
        lambda *refs: prepare_kernel(half, *refs),
        [
            jax.ShapeDtypeStruct((modes * half, TAIL), BF16),
            pltpu.HBM(((modes - KEPT) * half, 2 * LANES), BF16),
            jax.ShapeDtypeStruct((KEPT * half, 2 * LANES), BF16),
        ],
        [
            *[pltpu.VMEM((2, 2 * half, pairs), BF16)] * 2,
            pltpu.VMEM(((modes - KEPT) * half, 2 * LANES), BF16),
            pltpu.SemaphoreType.DMA((modes - KEPT,)),
        ],
        out_specs=[vmem, hbm, vmem],
    )(*tables)
    partial, other = call(
        lambda *refs: apply_kernel(own, *refs),
        [jax.ShapeDtypeStruct((half, LANES), F32)] * 2,
        [
            pltpu.VMEM(((modes - KEPT) * half, 2 * LANES), BF16),
            pltpu.VMEM((parts * unit + 8, LANES), F32),
            pltpu.VMEM((slots, half + 8, LANES), F32),
            pltpu.VMEM((modes, 4 * rows, half), BF16),
            pltpu.SemaphoreType.DMA((PIECES,)),
        ],
        in_specs=[smem] + [vmem] * 5 + [hbm],
    )(where, got, theirs, mine, coupling, kept, in_hbm(rest))
    other = lax.ppermute(other, "core", swap)
    finished = call(
        lambda *refs: finish_kernel(own, *refs),
        jax.ShapeDtypeStruct((parts, 8, LANES), BF16),
        [pltpu.VMEM((half + 8, LANES), F32)],
    )(partial, other)
    returned = lax.all_to_all(finished, "chip", 0, 0, tiled=True)
    out = call(
        deliver_kernel, jax.ShapeDtypeStruct((own, nodes, block), BF16), [pltpu.VMEM((nodes * 8, LANES), F32)]
    )(returned)
    return jnp.transpose(out, (1, 2, 0))


def solution(mesh):
    chaos, meshes = mesh.devices.shape
    chips = Mesh(mesh.devices.reshape(chaos // 2, 2, meshes), ("chip", "core", "mesh"))
    spread = ("chip", "core")
    return jax.shard_map(
        compute,
        mesh=chips,
        in_specs=(
            P("mesh", None, spread),
            P(None, ("mesh", *spread), None, None),
            P("mesh", None),
            P(),
            P(),
            P(),
        ),
        out_specs=P("mesh", None, spread),
        check_vma=False,
    )
```

```python
import jax
import jax.numpy as jnp
from jax import lax
from jax.experimental import pallas as pl
from jax.experimental.pallas import tpu as pltpu
from jax.sharding import Mesh, PartitionSpec as P


LANES = 128
BF16 = jnp.bfloat16
F32 = jnp.float32


def split_two(value):
    high = value.astype(BF16)
    return high, (value - high.astype(F32)).astype(BF16)


def call(body, outs, scratch=(), vmem=12, **specs):
    return pl.pallas_call(
        body,
        out_shape=outs,
        scratch_shapes=scratch,
        compiler_params=pltpu.CompilerParams(vmem_limit_bytes=vmem << 20),
        **specs,
    )


def in_hbm(array):
    return pltpu.with_memory_space_constraint(array, pltpu.HBM)


TAIL = 3 * LANES
PIECES = 5
KEPT = 1
NT = (((1,), (1,)), ((), ()))


def sublane_iota(count, width):
    return lax.broadcasted_iota(jnp.int32, (count, width), 0).astype(F32).astype(BF16)


def prepare_kernel(half, near_ref, far_ref, cols_ref, high_ref, low_ref, out_ref, rest_hbm, kept_ref, every_row, weights, rest, sem):
    modes, pairs = cols_ref.shape
    one, zero = jnp.ones((), BF16), jnp.zeros((), BF16)
    iota = sublane_iota(half, pairs)
    stores = []
    for mode in range(modes):
        at, slot = slice(mode, mode + 1), mode % 2
        hit = iota == cols_ref[at, :]
        weights[slot, :half, :] = jnp.where(hit, high_ref[at, :], zero)
        weights[slot, half:, :] = jnp.where(hit, low_ref[at, :], zero)
        for side, ref in enumerate((near_ref, far_ref)):
            every_row[slot, side * half : (side + 1) * half, :] = jnp.where(iota == ref[at, :], one, zero)
        got = lax.dot_general(weights[slot], every_row[slot], NT, preferred_element_type=F32)
        high, low = split_two(got[:half] + got[half:])
        lines = slice(mode * half, (mode + 1) * half)
        out_ref[lines, : 2 * half] = high
        out_ref[lines, 2 * half :] = low[:, 2 * LANES :]
        if mode >= modes - KEPT:
            kept = mode - modes + KEPT
            kept_ref[kept * half : (kept + 1) * half, :] = low[:, : 2 * LANES]
            continue
        rest[lines, :] = low[:, : 2 * LANES]
        store = pltpu.make_async_copy(rest.at[lines], rest_hbm.at[lines], sem.at[mode])
        store.start()
        stores.append(store)
    for store in stores:
        store.wait()


def tables_kernel(own, *refs):
    (held_hbm, *tables_hbm), (held_ref, out_ref, near_ref, far_ref, at_ref, high_ref, low_ref) = refs[:5], refs[5:12]
    columns_ref, rows_ref, cols_ref, vals_ref, table, sem = refs[12:]
    targets = (columns_ref, rows_ref, cols_ref, vals_ref, held_ref)
    loads = [
        pltpu.make_async_copy(hbm, target, sem.at[at])
        for at, (hbm, target) in enumerate(zip((*tables_hbm, held_hbm), targets))
    ]
    for load in loads:
        load.start()
    for load in loads:
        load.wait()
    me, core = lax.axis_index("mesh"), lax.axis_index("core")
    slots, nodes = columns_ref.shape
    columns = columns_ref[...]
    bits = nodes.bit_length() - 1
    away = jnp.bitwise_and(me - jnp.right_shift(columns, bits), LANES // nodes - 1)
    place = away * nodes + jnp.bitwise_and(columns, nodes - 1)
    table[...] = jnp.zeros_like(table)
    table[:slots, :nodes] = place.astype(F32)
    upright = table[...].T
    lanes = lax.broadcasted_iota(jnp.int32, (nodes, LANES), 1).astype(F32)
    for slot in range(slots):
        hit = upright[:nodes, slot : slot + 1] == lanes
        out_ref[slot * nodes : (slot + 1) * nodes, :] = jnp.where(hit, 1.0, 0.0).astype(BF16)

    def share(index):
        part = jnp.right_shift(index * (65536 // (2 * own) + 1), 16)
        rest = index - part * (2 * own)
        other = jnp.where(rest >= own, 1, 0)
        return (part * own + rest - other * own).astype(F32), other == core

    row_at, row_mine = share(rows_ref[...])
    col_at, col_mine = share(cols_ref[...])
    near_ref[...] = jnp.where(row_mine, row_at, -1.0).astype(BF16)
    far_ref[...] = jnp.where(row_mine, -1.0, row_at).astype(BF16)
    at_ref[...] = jnp.where(col_mine, col_at, -1.0).astype(BF16)
    high_ref[...], low_ref[...] = split_two(vals_ref[...])


def send_kernel(unit, select_ref, a_ref, b_ref, c_ref, d_ref, out_ref, held, wide):
    own, nodes, block = a_ref.shape
    slots = select_ref.shape[0] // nodes
    held[...] = jnp.zeros_like(held)
    for ref_at, ref in enumerate((a_ref, b_ref, c_ref, d_ref)):
        for i in range(own):
            held[i, ref_at * nodes : (ref_at + 1) * nodes, :block] = ref[i]
    select = select_ref[...]
    for i in range(own):
        got = jnp.dot(select, held[i], preferred_element_type=F32)
        for slot in range(slots):
            wide[pl.ds(own * slot + i, nodes, stride=unit), :] = got[slot * nodes : (slot + 1) * nodes]
    for line in range(own * slots, unit):
        wide[pl.ds(line, nodes, stride=unit), :] = jnp.zeros((nodes, LANES), F32)
    out_ref[...] = wide[...].astype(BF16)


def apply_kernel(own, got_ref, theirs_ref, mine_ref, coupling_ref, kept_ref, rest_hbm, near_ref, far_ref, rest, wide, slotted, stack, sem):
    pieces = sem.shape[0]
    length = rest.shape[0] // pieces

    def load(piece):
        at = pl.ds(pl.multiple_of(piece * length, 16), length)
        return pltpu.make_async_copy(rest_hbm.at[at], rest.at[at], sem.at[piece])

    @pl.loop(0, pieces)
    def _(piece):
        load(piece).start()

    core = lax.axis_index("core")
    parts, unit, _ = got_ref.shape
    modes, slots, rows, block = mine_ref.shape
    half = own * parts
    wide[: parts * unit, :] = got_ref[...].reshape(parts * unit, LANES).astype(F32)
    wide[parts * unit :, :] = jnp.zeros((8, LANES), F32)
    for slot in range(slots):
        for part in range(parts):
            slotted[slot, pl.ds(own * part, 8), :] = wide[pl.ds(unit * part + own * slot, 8), :]
    held = [slotted[slot, :half, :block].astype(BF16) for slot in range(slots)]
    for ref, part in ((theirs_ref, 1 - core), (mine_ref, core)):
        products = jnp.zeros((modes * rows, half), F32)
        for slot in range(slots):
            lines = ref[:, slot].reshape(modes * rows, block)
            products += lax.dot_general(lines, held[slot], NT, preferred_element_type=F32)
        start = pl.multiple_of(part * rows, 16)
        for mode in range(modes):
            high, low = split_two(products[mode * rows : (mode + 1) * rows])
            stack[mode, pl.ds(start, rows), :] = high
            stack[mode, pl.ds(2 * rows + start, rows), :] = low
    first = jnp.zeros((4 * rows, TAIL), F32)
    second = jnp.zeros((2 * rows, 2 * LANES), F32)
    for mode in range(modes):
        lines = slice(mode * half, (mode + 1) * half)
        first += jnp.dot(stack[mode], coupling_ref[lines, :], preferred_element_type=F32)
    for kept in range(KEPT):
        low = kept_ref[kept * half : (kept + 1) * half, :]
        second += jnp.dot(stack[modes - KEPT + kept, : 2 * rows], low, preferred_element_type=F32)
    for piece in range(pieces):
        load(piece).wait()
    for mode in range(modes - KEPT):
        low = rest[mode * half : (mode + 1) * half, :]
        second += jnp.dot(stack[mode, : 2 * rows], low, preferred_element_type=F32)
    both = first[: 2 * rows] + first[2 * rows :]
    tail = first[: 2 * rows, 2 * half :]
    total = jnp.concatenate([both[:, : 2 * LANES] + second, both[:, 2 * LANES : 2 * half] + tail], axis=1)
    edge = jnp.zeros((2 * rows, TAIL - 2 * half), F32)
    upright = jnp.concatenate([total, edge], axis=1).T
    near_ref[:, : 2 * rows] = upright[:half]
    far_ref[:, : 2 * rows] = upright[half : 2 * half]
    near_ref[:, 2 * rows :] = jnp.zeros((half, LANES - 2 * rows), F32)
    far_ref[:, 2 * rows :] = jnp.zeros((half, LANES - 2 * rows), F32)


def finish_kernel(own, mine_ref, other_ref, out_ref, total):
    parts = out_ref.shape[0]
    half = own * parts
    total[:half, :] = mine_ref[...] + other_ref[...]
    total[half:, :] = jnp.zeros((8, LANES), F32)
    for part in range(parts):
        out_ref[part] = total[pl.ds(own * part, 8), :].astype(BF16)


def deliver_kernel(got_ref, out_ref, wide):
    own, nodes, block = out_ref.shape
    wide[...] = got_ref[...].reshape(nodes * 8, LANES).astype(F32)
    for i in range(own):
        out_ref[i] = wide[pl.ds(i, nodes, stride=8), :][:, :block].astype(BF16)


def compute(coefficients, stiffness, columns, pair_rows, pair_cols, pair_vals):
    nodes, block, own = coefficients.shape
    modes, rows, slots, _ = stiffness.shape
    pairs = pair_rows.shape[1]
    parts = lax.axis_size("chip")
    meshes = lax.axis_size("mesh")
    half = own * parts
    unit = 32

    swap = [(0, 1), (1, 0)]
    held = jnp.transpose(coefficients, (2, 0, 1))
    around = {}
    for d in (2, 1, 3):
        around[d] = lax.ppermute(held, "mesh", [(i, (i + d) % meshes) for i in range(meshes)])
    vmem = pl.BlockSpec(memory_space=pltpu.VMEM)
    hbm = pl.BlockSpec(memory_space=pltpu.HBM)
    entries = jax.ShapeDtypeStruct((modes, pairs), BF16)
    held, select, *tables = call(
        lambda *refs: tables_kernel(own, *refs),
        [jax.ShapeDtypeStruct(held.shape, BF16), jax.ShapeDtypeStruct((slots * nodes, LANES), BF16)] + [entries] * 5,
        [pltpu.VMEM((slots, nodes), jnp.int32)]
        + [pltpu.VMEM((modes, pairs), x.dtype) for x in (pair_rows, pair_cols, pair_vals)]
        + [pltpu.VMEM((8, LANES), F32), pltpu.SemaphoreType.DMA((5,))],
        in_specs=[hbm] * 5,
    )(*map(in_hbm, (held, columns.T, pair_rows, pair_cols, pair_vals)))
    outgoing = call(
        lambda *refs: send_kernel(unit, *refs),
        jax.ShapeDtypeStruct((parts * unit, LANES), BF16),
        [pltpu.VMEM((own, LANES, LANES), BF16), pltpu.VMEM((parts * unit, LANES), F32)],
    )(select, held, *(around[d] for d in (1, 2, 3)))
    got = lax.all_to_all(outgoing.reshape(parts, unit, LANES), "chip", 0, 0, tiled=True)

    mine = jnp.transpose(stiffness, (0, 2, 1, 3))
    theirs = lax.ppermute(mine, "core", swap)
    coupling, rest, kept = call(
        lambda *refs: prepare_kernel(half, *refs),
        [
            jax.ShapeDtypeStruct((modes * half, TAIL), BF16),
            pltpu.HBM(((modes - KEPT) * half, 2 * LANES), BF16),
            jax.ShapeDtypeStruct((KEPT * half, 2 * LANES), BF16),
        ],
        [
            *[pltpu.VMEM((2, 2 * half, pairs), BF16)] * 2,
            pltpu.VMEM(((modes - KEPT) * half, 2 * LANES), BF16),
            pltpu.SemaphoreType.DMA((modes - KEPT,)),
        ],
        out_specs=[vmem, hbm, vmem],
    )(*tables)
    partial, other = call(
        lambda *refs: apply_kernel(own, *refs),
        [jax.ShapeDtypeStruct((half, LANES), F32)] * 2,
        [
            pltpu.VMEM(((modes - KEPT) * half, 2 * LANES), BF16),
            pltpu.VMEM((parts * unit + 8, LANES), F32),
            pltpu.VMEM((slots, half + 8, LANES), F32),
            pltpu.VMEM((modes, 4 * rows, half), BF16),
            pltpu.SemaphoreType.DMA((PIECES,)),
        ],
        in_specs=[vmem] * 5 + [hbm],
    )(got, theirs, mine, coupling, kept, in_hbm(rest))
    other = lax.ppermute(other, "core", swap)
    finished = call(
        lambda *refs: finish_kernel(own, *refs),
        jax.ShapeDtypeStruct((parts, 8, LANES), BF16),
        [pltpu.VMEM((half + 8, LANES), F32)],
    )(partial, other)
    returned = lax.all_to_all(finished, "chip", 0, 0, tiled=True)
    out = call(
        deliver_kernel, jax.ShapeDtypeStruct((own, nodes, block), BF16), [pltpu.VMEM((nodes * 8, LANES), F32)]
    )(returned)
    return jnp.transpose(out, (1, 2, 0))


def solution(mesh):
    chaos, meshes = mesh.devices.shape
    chips = Mesh(mesh.devices.reshape(chaos // 2, 2, meshes), ("chip", "core", "mesh"))
    spread = ("chip", "core")
    return jax.shard_map(
        compute,
        mesh=chips,
        in_specs=(
            P("mesh", None, spread),
            P(None, ("mesh", *spread), None, None),
            P("mesh", None),
            P(),
            P(),
            P(),
        ),
        out_specs=P("mesh", None, spread),
        check_vma=False,
    )
```

```python
import jax
import jax.numpy as jnp
from jax import lax
from jax.experimental import pallas as pl
from jax.experimental.pallas import tpu as pltpu
from jax.sharding import Mesh, PartitionSpec as P


LANES = 128
BF16 = jnp.bfloat16
F32 = jnp.float32


def split_two(value):
    high = value.astype(BF16)
    return high, (value - high.astype(F32)).astype(BF16)


def call(body, outs, scratch=(), vmem=12, **specs):
    return pl.pallas_call(
        body,
        out_shape=outs,
        scratch_shapes=scratch,
        compiler_params=pltpu.CompilerParams(vmem_limit_bytes=vmem << 20),
        **specs,
    )


def in_hbm(array):
    return pltpu.with_memory_space_constraint(array, pltpu.HBM)


TAIL = 3 * LANES
EARLY = 2
PIECES = 7
KEPT = 2
NT = (((1,), (1,)), ((), ()))


def sublane_iota(count, width):
    return lax.broadcasted_iota(jnp.int32, (count, width), 0).astype(F32).astype(BF16)


def prepare_kernel(half, chosen, kept_modes, near_ref, far_ref, cols_ref, high_ref, low_ref, out_ref, rest_hbm, *refs):
    *kept_ref, every_row, weights, rest, sem = refs
    modes, pairs = len(chosen), cols_ref.shape[1]
    one, zero = jnp.ones((), BF16), jnp.zeros((), BF16)
    iota = sublane_iota(half, pairs)
    stores = []
    for mode in range(modes):
        at, slot = slice(chosen[mode], chosen[mode] + 1), mode % 2
        hit = iota == cols_ref[at, :]
        weights[slot, :half, :] = jnp.where(hit, high_ref[at, :], zero)
        weights[slot, half:, :] = jnp.where(hit, low_ref[at, :], zero)
        for side, ref in enumerate((near_ref, far_ref)):
            every_row[slot, side * half : (side + 1) * half, :] = jnp.where(iota == ref[at, :], one, zero)
        got = lax.dot_general(weights[slot], every_row[slot], NT, preferred_element_type=F32)
        high, low = split_two(got[:half] + got[half:])
        lines = slice(mode * half, (mode + 1) * half)
        out_ref[lines, : 2 * half] = high
        out_ref[lines, 2 * half :] = low[:, 2 * LANES :]
        if mode >= modes - kept_modes:
            kept = mode - modes + kept_modes
            kept_ref[0][kept * half : (kept + 1) * half, :] = low[:, : 2 * LANES]
            continue
        rest[lines, :] = low[:, : 2 * LANES]
        store = pltpu.make_async_copy(rest.at[lines], rest_hbm.at[lines], sem.at[mode])
        store.start()
        stores.append(store)
    for store in stores:
        store.wait()


def tables_kernel(own, parts, *refs):
    (held_hbm, *tables_hbm), (held_ref, out_ref, near_ref, far_ref, at_ref, high_ref, low_ref) = refs[:5], refs[5:12]
    columns_ref, rows_ref, cols_ref, vals_ref, table, sem = refs[12:]
    targets = (columns_ref, rows_ref, cols_ref, vals_ref, held_ref)
    loads = [
        pltpu.make_async_copy(hbm, target, sem.at[at])
        for at, (hbm, target) in enumerate(zip((*tables_hbm, held_hbm), targets))
    ]
    for load in loads:
        load.start()
    for load in loads:
        load.wait()
    me, core = lax.axis_index("mesh"), lax.axis_index("core")
    slots, nodes = columns_ref.shape
    columns = columns_ref[...]
    bits = nodes.bit_length() - 1
    away = jnp.bitwise_and(me - jnp.right_shift(columns, bits), LANES // nodes - 1)
    place = away * nodes + jnp.bitwise_and(columns, nodes - 1)
    table[...] = jnp.zeros_like(table)
    table[:slots, :nodes] = place.astype(F32)
    upright = table[...].T
    lanes = lax.broadcasted_iota(jnp.int32, (nodes, LANES), 1).astype(F32)
    for slot in range(slots):
        hit = upright[:nodes, slot : slot + 1] == lanes
        out_ref[slot * nodes : (slot + 1) * nodes, :] = jnp.where(hit, 1.0, 0.0).astype(BF16)

    def share(index, part_step, own_step):
        part = jnp.right_shift(index * (65536 // (2 * own) + 1), 16)
        rest = index - part * (2 * own)
        other = jnp.where(rest >= own, 1, 0)
        return (part * part_step + (rest - other * own) * own_step).astype(F32), other == core

    row_at, row_mine = share(rows_ref[...], own, 1)
    col_at, col_mine = share(cols_ref[...], 1, parts)
    near_ref[...] = jnp.where(row_mine, row_at, -1.0).astype(BF16)
    far_ref[...] = jnp.where(row_mine, -1.0, row_at).astype(BF16)
    at_ref[...] = jnp.where(col_mine, col_at, -1.0).astype(BF16)
    high_ref[...], low_ref[...] = split_two(vals_ref[...])


def lane_ids(count):
    return lax.broadcasted_iota(jnp.int32, (count, LANES), 1)


def tail_place(own, slots, slot, i):
    first = own * slots // 2
    if i < 4:
        return first + slot, 32 * i
    return first + slots + slot // 4, 32 * (slot % 4)


def send_kernel(unit, select_ref, a_ref, b_ref, c_ref, d_ref, out_ref, held, wide):
    own, nodes, block = a_ref.shape
    slots = select_ref.shape[0] // nodes
    held[...] = jnp.zeros_like(held)
    for ref_at, ref in enumerate((a_ref, b_ref, c_ref, d_ref)):
        for i in range(own):
            held[i, ref_at * nodes : (ref_at + 1) * nodes, :block] = ref[i]
    select = select_ref[...]
    lanes = lane_ids(nodes)
    tails = {}
    for i in range(own):
        got = jnp.dot(select, held[i], preferred_element_type=F32)
        of = [got[slot * nodes : (slot + 1) * nodes] for slot in range(slots)]
        for slot in range(slots // 2):
            both = jnp.where(lanes < 64, of[slot], pltpu.roll(of[slot + slots // 2], 64, 1))
            wide[pl.ds(own * slot + i, nodes, stride=unit), :] = both
        for slot in range(slots):
            line, lane = tail_place(own, slots, slot, i)
            moved = of[slot] if lane == 64 else pltpu.roll(of[slot], (lane - 64) % LANES, 1)
            so_far = tails.get(line, jnp.zeros((nodes, LANES), F32))
            tails[line] = jnp.where((lanes >= lane) & (lanes < lane + 32), moved, so_far)
    for line in range(own * slots // 2, unit):
        wide[pl.ds(line, nodes, stride=unit), :] = tails.get(line, jnp.zeros((nodes, LANES), F32))
    out_ref[...] = wide[...].astype(BF16)


def apply_kernel(own, early, got_ref, theirs_ref, mine_ref, early_ref, late_ref, kept_ref, early_hbm, late_hbm, near_ref, far_ref, *refs):
    early_rest, rest, wide, slotted, stack, early_sem, sem = refs
    pieces = sem.shape[0]
    length = rest.shape[0] // pieces
    early_load = pltpu.make_async_copy(early_hbm, early_rest, early_sem.at[0])

    def load(piece):
        at = pl.ds(pl.multiple_of(piece * length, 16), length)
        return pltpu.make_async_copy(late_hbm.at[at], rest.at[at], sem.at[piece])

    early_load.start()

    @pl.loop(0, pieces)
    def _(piece):
        load(piece).start()

    core = lax.axis_index("core")
    parts, unit, _ = got_ref.shape
    modes, slots, rows, block = mine_ref.shape
    half = own * parts
    wide[...] = got_ref[...].reshape(parts * unit, LANES).astype(F32)
    lanes = lane_ids(parts)

    def line(at):
        return wide[pl.ds(at, parts, stride=unit), :]

    for i in range(own):
        for slot in range(slots // 2):
            both = line(own * slot + i)
            for to, main in ((slot, both), (slot + slots // 2, pltpu.roll(both, 64, 1))):
                at, lane = tail_place(own, slots, to, i)
                tail = line(at) if lane == 64 else pltpu.roll(line(at), (64 - lane) % LANES, 1)
                slotted[to, i * parts : (i + 1) * parts, :] = jnp.where(lanes < 64, main, tail).astype(BF16)
    held = [slotted[slot, :, :block] for slot in range(slots)]
    for ref, part in ((theirs_ref, 1 - core), (mine_ref, core)):
        products = jnp.zeros((modes * rows, half), F32)
        for slot in range(slots):
            lines = ref[:, slot].reshape(modes * rows, block)
            products += lax.dot_general(lines, held[slot], NT, preferred_element_type=F32)
        start = pl.multiple_of(part * rows, 16)
        for mode in range(modes):
            high, low = split_two(products[mode * rows : (mode + 1) * rows])
            stack[mode, pl.ds(start, rows), :] = high
            stack[mode, pl.ds(2 * rows + start, rows), :] = low
    first = jnp.zeros((4 * rows, TAIL), F32)
    second = jnp.zeros((2 * rows, 2 * LANES), F32)
    for mode in range(modes):
        ref, at = (early_ref, mode) if mode < early else (late_ref, mode - early)
        first += jnp.dot(stack[mode], ref[at * half : (at + 1) * half, :], preferred_element_type=F32)

    def add_low(mode, low):
        return second + jnp.dot(stack[mode, : 2 * rows], low, preferred_element_type=F32)

    kept_modes = kept_ref.shape[0] // half
    for at in range(kept_modes):
        second = add_low(modes - kept_modes + at, kept_ref[at * half : (at + 1) * half, :])
    early_load.wait()
    for mode in range(early):
        second = add_low(mode, early_rest[mode * half : (mode + 1) * half, :])
    for piece in range(pieces):
        load(piece).wait()
    for at in range(modes - kept_modes - early):
        second = add_low(early + at, rest[at * half : (at + 1) * half, :])
    both = first[: 2 * rows] + first[2 * rows :]
    tail = first[: 2 * rows, 2 * half :]
    total = jnp.concatenate([both[:, : 2 * LANES] + second, both[:, 2 * LANES : 2 * half] + tail], axis=1)
    edge = jnp.zeros((2 * rows, TAIL - 2 * half), F32)
    upright = jnp.concatenate([total, edge], axis=1).T
    near_ref[:, : 2 * rows] = upright[:half]
    far_ref[:, : 2 * rows] = upright[half : 2 * half]
    near_ref[:, 2 * rows :] = jnp.zeros((half, LANES - 2 * rows), F32)
    far_ref[:, 2 * rows :] = jnp.zeros((half, LANES - 2 * rows), F32)


def finish_kernel(own, mine_ref, other_ref, out_ref, total):
    parts = out_ref.shape[0]
    half = own * parts
    total[:half, :] = mine_ref[...] + other_ref[...]
    total[half:, :] = jnp.zeros((8, LANES), F32)
    for part in range(parts):
        out_ref[part] = total[pl.ds(own * part, 8), :].astype(BF16)


def deliver_kernel(got_ref, out_ref, wide):
    own, nodes, block = out_ref.shape
    wide[...] = got_ref[...].reshape(nodes * 8, LANES).astype(F32)
    for i in range(own):
        out_ref[i] = wide[pl.ds(i, nodes, stride=8), :][:, :block].astype(BF16)


def compute(coefficients, stiffness, columns, pair_rows, pair_cols, pair_vals):
    nodes, block, own = coefficients.shape
    modes, rows, slots, _ = stiffness.shape
    pairs = pair_rows.shape[1]
    parts = lax.axis_size("chip")
    meshes = lax.axis_size("mesh")
    half = own * parts
    unit = 24

    swap = [(0, 1), (1, 0)]
    held = jnp.transpose(coefficients, (2, 0, 1))
    around = {}
    for d in (2, 1, 3):
        around[d] = lax.ppermute(held, "mesh", [(i, (i + d) % meshes) for i in range(meshes)])
    vmem = pl.BlockSpec(memory_space=pltpu.VMEM)
    hbm = pl.BlockSpec(memory_space=pltpu.HBM)
    entries = jax.ShapeDtypeStruct((modes, pairs), BF16)
    held, select, *tables = call(
        lambda *refs: tables_kernel(own, parts, *refs),
        [jax.ShapeDtypeStruct(held.shape, BF16), jax.ShapeDtypeStruct((slots * nodes, LANES), BF16)] + [entries] * 5,
        [pltpu.VMEM((slots, nodes), jnp.int32)]
        + [pltpu.VMEM((modes, pairs), x.dtype) for x in (pair_rows, pair_cols, pair_vals)]
        + [pltpu.VMEM((8, LANES), F32), pltpu.SemaphoreType.DMA((5,))],
        in_specs=[hbm] * 5,
    )(*map(in_hbm, (held, columns.T, pair_rows, pair_cols, pair_vals)))
    outgoing = call(
        lambda *refs: send_kernel(unit, *refs),
        jax.ShapeDtypeStruct((parts * unit, LANES), BF16),
        [pltpu.VMEM((own, LANES, LANES), BF16), pltpu.VMEM((parts * unit, LANES), F32)],
    )(select, held, *(around[d] for d in (1, 2, 3)))
    got = lax.all_to_all(outgoing.reshape(parts, unit, LANES), "chip", 0, 0, tiled=True)

    mine = jnp.transpose(stiffness, (0, 2, 1, 3))
    theirs = lax.ppermute(mine, "core", swap)

    def prepare(chosen, kept_modes):
        count = len(chosen)
        sent = (count - kept_modes) * half
        kept_out = [jax.ShapeDtypeStruct((kept_modes * half, 2 * LANES), BF16)] if kept_modes else []
        return call(
            lambda *refs: prepare_kernel(half, chosen, kept_modes, *refs),
            [jax.ShapeDtypeStruct((count * half, TAIL), BF16), pltpu.HBM((sent, 2 * LANES), BF16)] + kept_out,
            [
                *[pltpu.VMEM((2, 2 * half, pairs), BF16)] * 2,
                pltpu.VMEM((sent, 2 * LANES), BF16),
                pltpu.SemaphoreType.DMA((count - kept_modes,)),
            ],
            out_specs=[vmem, hbm] + [vmem] * len(kept_out),
        )(*tables)

    early_coupling, early_rest = prepare(range(EARLY), 0)
    coupling, rest, kept = prepare(range(EARLY, modes), KEPT)
    partial, other = call(
        lambda *refs: apply_kernel(own, EARLY, *refs),
        [jax.ShapeDtypeStruct((half, LANES), F32)] * 2,
        [
            pltpu.VMEM(early_rest.shape, BF16),
            pltpu.VMEM(rest.shape, BF16),
            pltpu.VMEM((parts * unit, LANES), F32),
            pltpu.VMEM((slots, half, LANES), BF16),
            pltpu.VMEM((modes, 4 * rows, half), BF16),
            pltpu.SemaphoreType.DMA((1,)),
            pltpu.SemaphoreType.DMA((PIECES,)),
        ],
        in_specs=[vmem] * 6 + [hbm] * 2,
    )(got, theirs, mine, early_coupling, coupling, kept, in_hbm(early_rest), in_hbm(rest))
    other = lax.ppermute(other, "core", swap)
    finished = call(
        lambda *refs: finish_kernel(own, *refs),
        jax.ShapeDtypeStruct((parts, 8, LANES), BF16),
        [pltpu.VMEM((half + 8, LANES), F32)],
    )(partial, other)
    returned = lax.all_to_all(finished, "chip", 0, 0, tiled=True)
    out = call(
        deliver_kernel, jax.ShapeDtypeStruct((own, nodes, block), BF16), [pltpu.VMEM((nodes * 8, LANES), F32)]
    )(returned)
    return jnp.transpose(out, (1, 2, 0))


def solution(mesh):
    chaos, meshes = mesh.devices.shape
    chips = Mesh(mesh.devices.reshape(chaos // 2, 2, meshes), ("chip", "core", "mesh"))
    spread = ("chip", "core")
    return jax.shard_map(
        compute,
        mesh=chips,
        in_specs=(
            P("mesh", None, spread),
            P(None, ("mesh", *spread), None, None),
            P("mesh", None),
            P(),
            P(),
            P(),
        ),
        out_specs=P("mesh", None, spread),
        check_vma=False,
    )
```
